32 devices in a mesh: lines: 2 (over x), tile: 16 (over z, y, core).
Axes of the slice: x: 2, y: 2, z: 4, core: 2. Of those that a mesh axis runs over, the one named last changes fastest.
Arguments:
- traces: bfloat16 [1024, 512, 512], P(('lines', 'tile')), parts along dimension 0, may hold values from -6 to 6
Outputs:
- multiples: bfloat16 [1024, 512, 512], P(('lines', 'tile')), parts along dimension 0
The draws below stay inside these ranges and needn't reach their ends.
There are 2 independent parts, one for each index of `lines`. The reference program is written for one: setup_inputs(seed, part) draws one part's arguments, and reference() takes and returns one part's arrays. A program takes and returns all parts, laid end to end along the dimension named above; each array names one. Nothing has to cross between parts.
All inputs are finite; a program needn't handle non-finite values.
Results may differ from the reference program's by a relative error of at most 0.011.
Values may be sent and summed in bfloat16 or wider, within the bound.
A program may use at most 128 MiB of HBM per device.

```python
import math
import jax
import jax.numpy as jnp
from jax import lax

S = 512
NT = 512
F = 128


def level_of(rng, dims, shards, smallest, high):
    gain, own = 1.0, jax.random.fold_in(rng, 6)
    for dim, shards_of in shards:
        heights = jnp.exp(jax.random.uniform(jax.random.fold_in(own, dim), (shards_of,), jnp.float32, smallest / len(shards), high / len(shards)))
        gain = gain * jnp.repeat(heights, dims[dim] // shards_of).reshape([-1 if axis == dim else 1 for axis in range(len(dims))])
    return gain


def gaussian(own_key, extent, spread, reach, split=(), kind=jnp.bfloat16):
    entries = jax.random.normal(own_key, extent, jnp.float32) * spread
    if len(split) > 0:
        entries = level_of(own_key, extent, split, -0.22, 0.18) * entries
    return jnp.clip(entries, min=-reach, max=reach).astype(kind)


def setup_inputs(seed: int = 0, part: int = 0) -> dict:
    keys = jax.random.split(jax.random.key(seed), 2)
    part_splits = jax.random.split(jax.random.fold_in(keys[1], part), 2)
    return {
        "traces": gaussian(part_splits[0], (S, S, NT), 1.0, 6.0, ((0, 16),)),
    }


def make_tables():
    times = jnp.arange(NT, dtype=jnp.int32)
    freqs = jnp.arange(F, dtype=jnp.int32)
    phase = times[:, None] * freqs[None, :] % NT
    angle = phase.astype(jnp.float32) * (2.0 * math.pi / NT)
    norm = 1.0 / math.sqrt(NT)
    forward = jnp.stack([jnp.cos(angle), -jnp.sin(angle)], axis=-1).reshape(NT, 2 * F) * norm
    weight = jnp.where(freqs == 0, 1.0, 2.0).astype(jnp.float32)
    inverse = jnp.stack([jnp.cos(angle).T * weight[:, None], -jnp.sin(angle).T * weight[:, None]], axis=1)
    inverse = inverse.reshape(2 * F, NT) * norm
    return (forward.astype(jnp.bfloat16), inverse.astype(jnp.bfloat16))

def per_frequency(item):
    eta = 1.0 / math.sqrt(S)
    full = item.astype(jnp.float32)
    recorded = ((full + jnp.swapaxes(full, 1, 2)) * 0.5).astype(jnp.bfloat16)
    real_part = recorded[0].astype(jnp.float32)
    imag_part = recorded[1].astype(jnp.float32)

    def mult(a, b):
        return jnp.dot(a, b, precision=lax.Precision.HIGHEST)
    square_re = mult(real_part, real_part) - mult(imag_part, imag_part)
    square_im = mult(real_part, imag_part) + mult(imag_part, real_part)
    sum_re = (real_part + eta * square_re).astype(jnp.bfloat16)
    sum_im = (imag_part + eta * square_im).astype(jnp.bfloat16)
    sum_re = lax.optimization_barrier(sum_re).astype(jnp.float32)
    sum_im = lax.optimization_barrier(sum_im).astype(jnp.float32)
    pred_re = eta * (mult(real_part, sum_re) - mult(imag_part, sum_im))
    pred_im = eta * (mult(real_part, sum_im) + mult(imag_part, sum_re))
    return jnp.stack([pred_re, pred_im]).astype(jnp.bfloat16)

def reference(traces):
    forward, inverse = make_tables()
    spectrum = jnp.einsum('srt,tk->ksr', traces.astype(jnp.float32), forward.astype(jnp.float32), precision=lax.Precision.HIGHEST)
    spectrum = spectrum.astype(jnp.bfloat16).reshape(F, 2, S, S)
    predicted = lax.map(per_frequency, spectrum)
    flat = predicted.reshape(2 * F, S, S).astype(jnp.float32)
    multiples = jnp.einsum('ksr,kt->srt', flat, inverse.astype(jnp.float32), precision=lax.Precision.HIGHEST)
    return multiples.astype(jnp.bfloat16)
```

```python
import functools
import math

import jax
import jax.numpy as jnp
from jax import lax
from jax.experimental import pallas as pl
from jax.experimental.pallas import tpu as pltpu
from jax.sharding import PartitionSpec as P

S = 512
NT = 512
F = 128


def make_tables():
    times = jnp.arange(NT, dtype=jnp.int32)
    freqs = jnp.arange(F, dtype=jnp.int32)
    phase = times[:, None] * freqs[None, :] % NT
    angle = phase.astype(jnp.float32) * (2.0 * math.pi / NT)
    norm = 1.0 / math.sqrt(NT)
    forward = jnp.stack([jnp.cos(angle), -jnp.sin(angle)], axis=-1).reshape(NT, 2 * F) * norm
    weight = jnp.where(freqs == 0, 1.0, 2.0).astype(jnp.float32)
    inverse = jnp.stack(
        [jnp.cos(angle).T * weight[:, None], -jnp.sin(angle).T * weight[:, None]], axis=1
    )
    inverse = inverse.reshape(2 * F, NT) * norm
    return (forward.astype(jnp.bfloat16), inverse.astype(jnp.bfloat16))


def dot(left, right):
    return jnp.dot(left, right, preferred_element_type=jnp.float32)


def widen(value):
    return value.astype(jnp.float32)


def triangle(size):
    row = lax.broadcasted_iota(jnp.int32, (size, size), 0)
    column = lax.broadcasted_iota(jnp.int32, (size, size), 1)
    return row, column


def pack(full, where, tri_ref, diag_ref):
    size = full[0].shape[0] // 2
    row, column = triangle(size)
    diagonals = []
    for part in range(2):
        first = full[part][:size, :size]
        merged = jnp.where(row < column, first, full[part][size:, size:])
        tri_ref[where + (part, pl.ds(0, size))] = full[part][:size, size:].astype(jnp.bfloat16)
        tri_ref[where + (part, pl.ds(size, size))] = merged.astype(jnp.bfloat16)
        diagonals.append(jnp.sum(jnp.where(row == column, first, 0.0), axis=0, keepdims=True))
    lane = lax.broadcasted_iota(jnp.int32, (8, size), 0)
    both = jnp.where(lane == 0, diagonals[0], diagonals[1])
    diag_ref[where] = both.astype(jnp.bfloat16)


def unpack(tri, diagonal):
    size = tri.shape[1]
    row, column = triangle(size)
    upper = tri[:size]
    merged = tri[size:]
    turned = merged.T
    first = jnp.where(row == column, diagonal, jnp.where(row < column, merged, turned))
    last = jnp.where(row < column, turned, merged)
    return first, upper, upper.T, last


def exchange_kernel(
    count, ahead,
    x_ref, out_ref,
    rows_in, cross_in, raw, tri_out, diag_out, tri_in, diag_in, real_ref, imag_ref,
    pred_rows, pred_cross, ret_tri, ret_diag, got_tri, got_diag, spread,
    own_send, own_recv, own_copy, cross_send, cross_recv, raw_send, raw_recv, raw_copy,
    tri_send, tri_recv, diag_send, diag_recv,
    back_send, back_recv, back_copy, over_send, over_recv, pack_send, pack_recv, edge_send,
    edge_recv, fan_send, fan_recv, fan_copy,
):
    width = x_ref.shape[1]
    rows = x_ref.shape[3]
    half = count // 2
    quarter = count // 4
    span = half * rows
    me = lax.axis_index("tile")
    side = lax.div(me, half)
    mine = lax.rem(me, half)
    own0 = side * half
    other0 = (1 - side) * half
    own_cols = pl.ds(pl.multiple_of(side * span, span), span)
    other_cols = pl.ds(pl.multiple_of((1 - side) * span, span), span)
    is_relay = lax.div(mine, quarter) == 1 - side
    serves = lax.rem(mine, quarter)

    def relay_of(position, where):
        return quarter * (1 + where) + lax.rem(position, quarter)

    def remote(source, target, send_sem, recv_sem, peer):
        return pltpu.make_async_remote_copy(
            src_ref=source, dst_ref=target, send_sem=send_sem, recv_sem=recv_sem,
            device_id={"tile": peer}, device_id_type=pl.DeviceIdType.MESH,
        )

    def wait_bytes(view, sem):
        pltpu.make_async_copy(view, view, sem).wait()

    barrier = pltpu.get_barrier_semaphore()

    @pl.loop(1, count)
    def _(i):
        pl.semaphore_signal(
            barrier, inc=1, device_id={"tile": lax.rem(me + i, count)},
            device_id_type=pl.DeviceIdType.MESH,
        )

    pl.semaphore_wait(barrier, count - 1)

    def send_forward(f):
        @pl.loop(0, half)
        def _(i):
            position = lax.rem(mine + 3 * i, half)
            owner = other0 + position
            relay = relay_of(position, side)
            slot = lax.div(position, quarter)
            piece = x_ref.at[owner, f, :, :, own_cols]

            @pl.when(relay != me)
            def _():
                remote(piece, raw.at[slot, mine, f], raw_send.at[f], raw_recv.at[f], relay).start()

            @pl.when(relay == me)
            def _():
                pltpu.make_async_copy(piece, raw.at[slot, mine, f], raw_copy.at[slot, f]).start()

            remote(
                x_ref.at[owner, f, :, :, other_cols], cross_in.at[mine, f],
                cross_send.at[f], cross_recv.at[f], owner,
            ).start()

            near = own0 + position

            @pl.when(near != me)
            def _():
                remote(
                    x_ref.at[near, f], rows_in.at[mine, f], own_send.at[f], own_recv.at[f], near
                ).start()

            @pl.when(near == me)
            def _():
                pltpu.make_async_copy(x_ref.at[me, f], rows_in.at[mine, f], own_copy.at[f]).start()

    def relay_forward(f):
        for slot in range(2):
            pltpu.make_async_copy(
                raw.at[slot, mine, f], raw.at[slot, mine, f], raw_copy.at[slot, f]
            ).wait()
        wait_bytes(raw.at[pl.ds(0, 2), pl.ds(0, half - 1), f], raw_recv.at[f])

        @pl.loop(0, 2)
        def _(slot):
            full = []
            for part in range(2):
                value = widen(raw[slot, :, f, part]).reshape(span, span)
                full.append((value + value.T) * 0.5)
            pack(full, (slot, f), tri_out, diag_out)

        @pl.loop(0, 2)
        def _(slot):
            owner = other0 + slot * quarter + serves
            remote(
                tri_out.at[slot, f], tri_in.at[f], tri_send.at[f], tri_recv.at[f], owner
            ).start()
            remote(
                diag_out.at[slot, f], diag_in.at[f], diag_send.at[f], diag_recv.at[f], owner
            ).start()

    def predict(f):
        pltpu.make_async_copy(x_ref.at[me, f], rows_in.at[mine, f], own_copy.at[f]).wait()
        wait_bytes(rows_in.at[pl.ds(0, half - 1), f], own_recv.at[f])
        wait_bytes(cross_in.at[:, f], cross_recv.at[f])
        wait_bytes(tri_in.at[f], tri_recv.at[f])
        wait_bytes(diag_in.at[f], diag_recv.at[f])
        for part, target in ((0, real_ref), (1, imag_ref)):
            near = widen(rows_in[:, f, part, :, own_cols]).reshape(span, span)
            far = widen(rows_in[:, f, part, :, other_cols]).reshape(span, span)
            cross = widen(cross_in[:, f, part]).reshape(span, span)
            mixed = (far + cross.T) * 0.5
            first, upper, lower, last = unpack(
                widen(tri_in[f, part]), widen(diag_in[f])[part : part + 1]
            )
            half_span = span // 2
            target[:span, :span] = ((near + near.T) * 0.5).astype(jnp.bfloat16)
            target[:span, span:] = mixed.astype(jnp.bfloat16)
            target[span:, :span] = mixed.T.astype(jnp.bfloat16)
            target[span : span + half_span, span : span + half_span] = first.astype(jnp.bfloat16)
            target[span : span + half_span, span + half_span :] = upper.astype(jnp.bfloat16)
            target[span + half_span :, span : span + half_span] = lower.astype(jnp.bfloat16)
            target[span + half_span :, span + half_span :] = last.astype(jnp.bfloat16)
        eta = 1.0 / math.sqrt(S)
        real_part = real_ref[...]
        imag_part = imag_ref[...]
        square_re = dot(real_part, real_part) - dot(imag_part, imag_part)
        sum_re = (widen(real_part) + eta * square_re).astype(jnp.bfloat16)
        square_im = dot(real_part, imag_part) + dot(imag_part, real_part)
        sum_im = (widen(imag_part) + eta * square_im).astype(jnp.bfloat16)
        far_parts = []
        for part in range(2):
            if part == 0:
                value = eta * (dot(real_part, sum_re) - dot(imag_part, sum_im))
            else:
                value = eta * (dot(real_part, sum_im) + dot(imag_part, sum_re))
            far_parts.append(value[span:, span:])
            value = value.astype(jnp.bfloat16)
            pred_cross[:, f, part] = value[span:, :span].reshape(half, rows, span)
            pred_rows[:, f, part, :, own_cols] = value[:span, :span].reshape(half, rows, span)
            pred_rows[:, f, part, :, other_cols] = value[:span, span:].reshape(half, rows, span)
        pack(far_parts, (f,), ret_tri, ret_diag)

    def send_back(f):
        keep = pltpu.make_async_copy(pred_rows.at[mine, f], out_ref.at[me, f], back_copy.at[f])
        keep.start()
        keep.wait()
        relay = relay_of(mine, 1 - side)
        slot = lax.div(mine, quarter)
        remote(
            ret_tri.at[f], got_tri.at[slot, f], pack_send.at[f], pack_recv.at[f], relay
        ).start()
        remote(
            ret_diag.at[f], got_diag.at[slot, f], edge_send.at[f], edge_recv.at[f], relay
        ).start()

        @pl.loop(0, half)
        def _(i):
            position = lax.rem(mine + 3 * i, half)
            remote(
                pred_cross.at[position, f], out_ref.at[me, f, :, :, own_cols],
                over_send.at[f], over_recv.at[f], other0 + position,
            ).start()

            @pl.when(position != mine)
            def _():
                remote(
                    pred_rows.at[position, f], out_ref.at[me, f],
                    back_send.at[f], back_recv.at[f], own0 + position,
                ).start()

    def relay_back(f):
        wait_bytes(got_tri.at[:, f], pack_recv.at[f])
        wait_bytes(got_diag.at[:, f], edge_recv.at[f])

        @pl.loop(0, 2)
        def _(slot):
            for part in range(2):
                first, upper, lower, last = unpack(
                    widen(got_tri[slot, f, part]), widen(got_diag[slot, f])[part : part + 1]
                )
                top = jnp.concatenate([first, upper], axis=1)
                bottom = jnp.concatenate([lower, last], axis=1)
                full = jnp.concatenate([top, bottom], axis=0)
                spread[slot, :, f, part] = full.reshape(half, rows, span).astype(jnp.bfloat16)

        @pl.loop(0, 2)
        def _(slot):
            owner = other0 + slot * quarter + serves
            target = out_ref.at[owner, f, :, :, own_cols]

            @pl.loop(0, half)
            def _(i):
                position = lax.rem(mine + 3 * i, half)

                @pl.when(position != mine)
                def _():
                    remote(
                        spread.at[slot, position, f], target, fan_send.at[f], fan_recv.at[f],
                        own0 + position,
                    ).start()

                @pl.when(position == mine)
                def _():
                    pltpu.make_async_copy(
                        spread.at[slot, mine, f], target, fan_copy.at[slot, f]
                    ).start()

    @pl.loop(0, ahead)
    def _(f):
        send_forward(f)

    @pl.loop(0, width + 2)
    def _(i):
        @pl.when(i + ahead < width)
        def _():
            send_forward(i + ahead)

        @pl.when(jnp.logical_and(is_relay, i < width))
        def _():
            relay_forward(i)

        @pl.when(jnp.logical_and(i >= 1, i <= width))
        def _():
            predict(i - 1)
            send_back(i - 1)

        @pl.when(jnp.logical_and(is_relay, i >= 2))
        def _():
            relay_back(i - 2)

    @pl.loop(0, width)
    def _(f):
        wait_bytes(rows_in.at[pl.ds(0, half - 1), f], own_send.at[f])
        wait_bytes(cross_in.at[:, f], cross_send.at[f])
        wait_bytes(pred_rows.at[pl.ds(0, half - 1), f], back_send.at[f])
        wait_bytes(pred_rows.at[pl.ds(0, half - 1), f], back_recv.at[f])
        wait_bytes(pred_cross.at[:, f], over_send.at[f])
        wait_bytes(pred_cross.at[:, f], over_recv.at[f])
        wait_bytes(ret_tri.at[f], pack_send.at[f])
        wait_bytes(ret_diag.at[f], edge_send.at[f])

        @pl.when(is_relay)
        def _():
            wait_bytes(raw.at[0, pl.ds(0, half - 2), f], raw_send.at[f])
            wait_bytes(tri_out.at[:, f], tri_send.at[f])
            wait_bytes(diag_out.at[:, f], diag_send.at[f])
            wait_bytes(spread.at[:, pl.ds(0, half - 1), f], fan_send.at[f])
            wait_bytes(spread.at[0, pl.ds(0, half - 2), f], fan_recv.at[f])
            for slot in range(2):
                pltpu.make_async_copy(
                    spread.at[slot, mine, f], spread.at[slot, mine, f], fan_copy.at[slot, f]
                ).wait()

        @pl.when(jnp.logical_not(is_relay))
        def _():
            wait_bytes(raw.at[0, :, f], raw_send.at[f])
            wait_bytes(spread.at[0, :, f], fan_recv.at[f])


def exchange_and_predict(grouped, count):
    _, width, _, rows, _ = grouped.shape
    half = count // 2
    span = half * rows
    sems = pltpu.SemaphoreType.DMA((width,))
    pair = pltpu.SemaphoreType.DMA((2, width))

    def held(*shape):
        return pltpu.VMEM(shape, jnp.bfloat16)

    tri = (2, span, span // 2)
    diag = (8, span // 2)
    return pl.pallas_call(
        functools.partial(exchange_kernel, count, min(2, width)),
        in_specs=[pl.BlockSpec(memory_space=pl.ANY)],
        out_specs=pl.BlockSpec(memory_space=pl.ANY),
        out_shape=jax.ShapeDtypeStruct(grouped.shape, jnp.bfloat16),
        scratch_shapes=[
            held(half, width, 2, rows, S),
            held(half, width, 2, rows, span),
            held(2, half, width, 2, rows, span),
            held(2, width, *tri), held(2, width, *diag),
            held(width, *tri), held(width, *diag),
            held(S, S), held(S, S),
            held(half, width, 2, rows, S),
            held(half, width, 2, rows, span),
            held(width, *tri), held(width, *diag),
            held(2, width, *tri), held(2, width, *diag),
            held(2, half, width, 2, rows, span),
            sems, sems, sems, sems, sems, sems, sems, pair,
            sems, sems, sems, sems,
            sems, sems, sems, sems, sems, sems, sems, sems, sems, sems, sems, pair,
        ],
        compiler_params=pltpu.CompilerParams(
            collective_id=0, has_side_effects=True, vmem_limit_bytes=56 * 2**20
        ),
        cost_estimate=pl.CostEstimate(
            flops=width * 16 * S**3, bytes_accessed=width * 8 * S * S, transcendentals=0
        ),
        name="exchange_and_predict",
    )(grouped)


def local(traces):
    count = lax.axis_size("tile")
    rows = traces.shape[0]
    forward, inverse = make_tables()
    spectrum = jnp.einsum("srt,tk->ksr", traces, forward, preferred_element_type=jnp.float32)
    grouped = spectrum.astype(jnp.bfloat16).reshape(count, F // count, 2, rows, S)
    result = exchange_and_predict(grouped, count).reshape(2 * F, rows, S)
    multiples = jnp.einsum("kab,kt->abt", result, inverse, preferred_element_type=jnp.float32)
    return multiples.astype(jnp.bfloat16)


def solution(mesh):
    return jax.shard_map(
        local,
        mesh=mesh,
        in_specs=(P(("lines", "tile"), None, None),),
        out_specs=P(("lines", "tile"), None, None),
        check_vma=False,
    )
```
